32 devices in a mesh: groups: 2 (over y), dp: 16 (over z, x, core).
Axes of the slice: x: 2, y: 2, z: 4, core: 2. Of those that a mesh axis runs over, the one named last changes fastest.
Arguments:
- query_acts: bfloat16 [4096, 8192], P(('groups', 'dp')), parts along dimension 0, may hold values from -6 to 6
- cotangent: bfloat16 [4096, 8192], P(('groups', 'dp')), parts along dimension 0, may hold values from -6 to 6
- conv_weight: float32 [4, 4, 8192], replicated, may hold values from -3 to 3
- conv_bias: float32 [4, 8192], replicated, may hold values from -3 to 3
- owner_map: int32 [4], replicated, may hold values from 0 to 15, as said below
- basis_store: float32 [16, 25, 8192], P('dp'), may hold values from -2.5 to 2.5
- lambda_store: float32 [16, 5, 8192], P('dp'), may hold values from 0.1 to 10
- train_grads: bfloat16 [256, 4, 5, 8192], P(('groups', 'dp')), parts along dimension 0, may hold values from -6 to 6
- batch_index: int32 [512], P(('groups', 'dp')), parts along dimension 0, may hold values from 0 to 127, as said below
Outputs:
- adjoint_in: bfloat16 [4096, 8192], P(('groups', 'dp')), parts along dimension 0
- scores: float32 [512], P(('groups', 'dp')), parts along dimension 0
The draws below stay inside these ranges and needn't reach their ends.
There are 2 independent parts, one for each index of `groups`. The reference program is written for one: setup_inputs(seed, part) draws one part's arguments, and reference() takes and returns one part's arrays. A program takes and returns all parts, laid end to end along the dimension named above; an argument that names none is the same for every part. Nothing has to cross between parts.
Inputs may be any that keep to these rules, and one draw needn't show every extreme that they name: `owner_map`: the 4 entries are distinct. `batch_index`: entry n names a row from (n // 16) * 8 to (n // 16) * 8 + 7.
All inputs are finite; a program needn't handle non-finite values.
Results may differ from the reference program's by a relative error of at most 0.015.
Values may be sent and summed in bfloat16 or wider, within the bound.
A program may use at most 128 MiB of HBM per device.

```python
import math
import jax
import jax.numpy as jnp
from jax import lax

C = 8192
LAYERS = 4
E_DEV = 8
B_DEV = 16
TOKENS = 2048
TRAIN = 128
BATCH = 256
SLOTS = 16


def draw_owner_map(key, part):
    middle = jax.random.permutation(jax.random.fold_in(key, 1), SLOTS - 2)[:LAYERS - 2].astype(jnp.int32) + 1
    owners = jnp.concatenate([jnp.array([0, SLOTS - 1], dtype=jnp.int32), middle])
    order = jax.random.permutation(jax.random.fold_in(key, 2), LAYERS)
    return owners[order].astype(jnp.int32)


def draw_batch_index(key, part):
    base = jnp.arange(BATCH, dtype=jnp.int32) // B_DEV * E_DEV
    offsets = jax.random.randint(key, (BATCH,), 0, E_DEV, dtype=jnp.int32)
    offsets = offsets.at[0].set(0).at[BATCH - 1].set(E_DEV - 1)
    return (base + offsets).astype(jnp.int32)


def level_of(key, shape, pieces, least, largest):
    factor_of, own = 1.0, jax.random.fold_in(key, 6)
    for axis_at, blocks in pieces:
        steps = jnp.exp(jax.random.uniform(jax.random.fold_in(own, axis_at), (blocks,), jnp.float32, least / len(pieces), largest / len(pieces)))
        factor_of = factor_of * jnp.repeat(steps, shape[axis_at] // blocks).reshape([-1 if axis == axis_at else 1 for axis in range(len(shape))])
    return factor_of


def bell_draw(key, extent, scale, bound, split=(), kind=jnp.bfloat16):
    drawn = jax.random.normal(key, extent, jnp.float32) * scale
    if len(split) > 0:
        drawn = level_of(key, extent, split, -0.22, 0.18) * drawn
    return jnp.clip(drawn, min=-bound, max=bound).astype(kind)


def setup_inputs(seed: int = 0, part: int = 0) -> dict:
    splits = jax.random.split(jax.random.key(seed), 10)
    part_keys = jax.random.split(jax.random.fold_in(splits[9], part), 10)
    return {
        "query_acts": bell_draw(part_keys[0], (TOKENS, C), 1.0, 6.0, ((0, 16),)),
        "cotangent": bell_draw(part_keys[1], (TOKENS, C), 1.0, 6.0, ((0, 16),)),
        "conv_weight": bell_draw(splits[2], (LAYERS, 4, C), 4 ** -0.5, 3.0, (), jnp.float32),
        "conv_bias": bell_draw(splits[3], (LAYERS, C), 0.5, 3.0, (), jnp.float32),
        "owner_map": draw_owner_map(jax.random.fold_in(splits[9], 71), part),
        "basis_store": bell_draw(splits[5], (SLOTS, 25, C), 5 ** -0.5, 2.5, ((0, 16),), jnp.float32),
        "lambda_store": jnp.clip(jnp.exp(math.log(10.0) - 4.6051702 * jax.random.uniform(splits[6], (SLOTS, 5, C), jnp.float32) ** level_of(splits[6], (SLOTS, 5, C), ((0, 16),), -0.2, 0.2)), 0.1, 10.0),
        "train_grads": bell_draw(part_keys[7], (TRAIN, LAYERS, 5, C), 1.0, 6.0, ((0, 16),)),
        "batch_index": draw_batch_index(jax.random.fold_in(jax.random.fold_in(splits[9], part), 71), part),
    }


def convolve(padded, weights, bias, count):
    result = jnp.broadcast_to(bias[None, :], (count, bias.shape[0]))
    for offset in range(4):
        result = result + weights[offset][None, :] * padded[3 - offset:3 - offset + count].astype(jnp.float32)
    return result

def silu_slope(values):
    sig = jax.nn.sigmoid(values)
    return sig * (1.0 + values * (1.0 - sig))

def precondition(gradient, eigen_basis, eigen_vals):
    damping = 0.1 * jnp.mean(eigen_vals)
    rotated = lax.optimization_barrier(jnp.sum(eigen_basis * gradient[:, None, :], axis=0))
    scaled = rotated / (eigen_vals + damping)
    return lax.optimization_barrier(jnp.sum(eigen_basis * scaled[None, :, :], axis=1))

def window(acts, cot, weights, bias):
    count = acts.shape[0]
    width = acts.shape[1]
    stream = acts
    saved = []
    for layer_id in range(LAYERS):
        padded = jnp.concatenate([jnp.zeros((3, width), jnp.bfloat16), stream], axis=0)
        saved.append(padded)
        conv_out = convolve(padded, weights[layer_id], bias[layer_id], count)
        stream = (stream.astype(jnp.float32) + jax.nn.silu(conv_out)).astype(jnp.bfloat16)
    adjoint = cot
    partials = [None] * LAYERS
    for layer_id in reversed(range(LAYERS)):
        padded = saved[layer_id]
        conv_out = convolve(padded, weights[layer_id], bias[layer_id], count)
        conv_grad = (adjoint.astype(jnp.float32) * silu_slope(conv_out)).astype(jnp.bfloat16)
        grad_f = conv_grad.astype(jnp.float32)
        terms = [lax.optimization_barrier(jnp.sum(padded[3 - offset:3 - offset + count].astype(jnp.float32) * grad_f, axis=0)) for offset in range(4)]
        terms.append(lax.optimization_barrier(jnp.sum(grad_f, axis=0)))
        partials[layer_id] = jnp.stack(terms)
        extended = jnp.concatenate([conv_grad, jnp.zeros((3, width), jnp.bfloat16)], axis=0)
        conv_back = jnp.zeros((count, width), jnp.float32)
        for offset in range(4):
            conv_back = conv_back + weights[layer_id, offset][None, :] * extended[offset:offset + count].astype(jnp.float32)
        adjoint = (adjoint.astype(jnp.float32) + conv_back).astype(jnp.bfloat16)
    return (adjoint, jnp.stack(partials))

def reference(query_acts, cotangent, conv_weight, conv_bias, owner_map, basis_store, lambda_store, train_grads, batch_index):
    width = 128
    blocks = C // width
    acts_blocks = query_acts.reshape(TOKENS, blocks, width).transpose(1, 0, 2)
    cot_blocks = cotangent.reshape(TOKENS, blocks, width).transpose(1, 0, 2)
    weight_blocks = conv_weight.reshape(LAYERS, 4, blocks, width).transpose(2, 0, 1, 3)
    bias_blocks = conv_bias.reshape(LAYERS, blocks, width).transpose(1, 0, 2)
    adjoint_blocks, grad_blocks = lax.map(lambda packed: window(packed[0], packed[1], packed[2], packed[3]), (acts_blocks, cot_blocks, weight_blocks, bias_blocks))
    adjoint_in = adjoint_blocks.transpose(1, 0, 2).reshape(TOKENS, C)
    gradients = grad_blocks.transpose(1, 2, 0, 3).reshape(LAYERS, 5, C) * (1.0 / math.sqrt(TOKENS))
    corrected = []
    for layer_id in range(LAYERS):
        owner = owner_map[layer_id]
        eigen_basis = basis_store[owner].reshape(5, 5, C)
        eigen_vals = lambda_store[owner]
        corrected.append(precondition(gradients[layer_id], eigen_basis, eigen_vals))
    flattened = jnp.stack(corrected).reshape(-1)
    high_part = flattened.astype(jnp.bfloat16)
    low_part = (flattened - high_part.astype(jnp.float32)).astype(jnp.bfloat16)
    both_parts = jnp.stack([high_part, low_part], axis=1).astype(jnp.float32)
    rows_view = train_grads.reshape(SLOTS, E_DEV, LAYERS * 5 * C)
    all_scores = lax.map(lambda block_rows: lax.optimization_barrier(jnp.sum(jnp.dot(block_rows.astype(jnp.float32), both_parts, precision=lax.Precision.HIGHEST), axis=1)), rows_view).reshape(TRAIN)
    all_scores = all_scores * (1.0 / math.sqrt(5 * LAYERS * C))
    scores = all_scores[batch_index]
    return (adjoint_in, scores)
```

```python
import functools
import math

import jax
import jax.numpy as jnp
import numpy as np
from jax import lax
from jax.experimental import pallas as pl
from jax.experimental.pallas import tpu as pltpu
from jax.sharding import PartitionSpec as P

LANES = 128
SUB = 8
TAPS = 4
HALO_ROWS = 16
PAIRS = [(j, k) for j in range(5) for k in range(j, 5)]


def layout_plan(rows, layers):
    reach = (TAPS - 1) * layers
    extended = rows + 2 * reach
    fold = -(-extended // SUB)
    padded = -(-(fold * SUB) // 16) * 16
    return reach, fold, padded


def permutations(rows, layers):
    reach, fold, padded = layout_plan(rows, layers)
    columns = rows + 2 * HALO_ROWS
    into = np.zeros((padded, columns), np.float32)
    back = np.zeros((rows, padded), np.float32)
    for j in range(fold):
        for s in range(SUB):
            token = fold * s + j - reach
            row = SUB * j + s
            if 0 <= token < rows:
                into[row, token] = 1.0
                back[token, row] = 1.0
            elif -reach <= token < 0:
                into[row, rows + HALO_ROWS + token] = 1.0
            elif rows <= token < rows + reach:
                into[row, HALO_ROWS + token] = 1.0
    return jnp.asarray(into, jnp.bfloat16), jnp.asarray(back, jnp.bfloat16)


def rounded(value):
    return value.astype(jnp.bfloat16).astype(jnp.float32)


def window_chunk(lanes, rows, layers, is_first, w_ref, b_ref, x_all, c_all, slope_all, g_ref):
    reach, fold, padded = layout_plan(rows, layers)
    sub = lax.broadcasted_iota(jnp.int32, (SUB, LANES), 0)
    edges = {}

    def own(j, low, high):
        tokens = [fold * s + j - reach for s in range(SUB)]
        inside = tuple(low <= t < high for t in tokens)
        if all(inside):
            return None
        if inside not in edges:
            lead = next(i for i, ok in enumerate(inside) if ok)
            tail = max(i for i, ok in enumerate(inside) if ok)
            edges[inside] = (sub >= lead) & (sub <= tail)
        return edges[inside]

    zero = jnp.zeros((SUB, LANES), jnp.float32)

    def keep(value, mask):
        return value if mask is None else jnp.where(mask, value, zero)

    def row(ref, *at):
        return jnp.broadcast_to(ref[at[:-1] + (pl.ds(at[-1], 1), lanes)], (SUB, LANES))

    live = {}

    def begun(j):
        mask = own(j, 0, 1 << 30)
        if mask is None:
            return None
        key = id(mask)
        if key not in live:
            live[key] = mask | jnp.logical_not(is_first)
        return live[key]

    last = TAPS - 1
    for layer in range(layers):
        taps = [row(w_ref, layer, k) * 0.5 for k in range(TAPS)]
        bias = row(b_ref, layer) * 0.5
        base = layer * (fold + last) * SUB
        for i in range(last):
            wrapped = x_all[pl.ds(base + (fold + i) * SUB, SUB), lanes]
            x_all[pl.ds(base + i * SUB, SUB), lanes] = pltpu.roll(wrapped, 1, 0)
        x = [x_all[pl.ds(base + i * SUB, SUB), lanes] for i in range(fold + last)]
        following = base + (fold + last + last) * SUB
        for j in range(fold):
            half = bias
            for k in range(TAPS):
                half = half + taps[k] * x[last + j - k]
            bent = jnp.tanh(half)
            up = 1.0 + bent
            slope_all[pl.ds((layer * fold + j) * SUB, SUB), lanes] = up * (1.0 + half * (1.0 - bent))
            if layer < layers - 1:
                fresh = keep(rounded(x[last + j] + half * up), begun(j))
                x_all[pl.ds(following + j * SUB, SUB), lanes] = fresh
    for layer in reversed(range(layers)):
        taps = [row(w_ref, layer, k) * 0.5 for k in range(TAPS)]
        base = layer * (fold + last) * SUB
        doubled = [None] * (fold + last)
        sums = [zero] * (TAPS + 1)

        def at(i):
            return x_all[pl.ds(base + i * SUB, SUB), lanes]

        for j in range(fold):
            adjoint = c_all[pl.ds(j * SUB, SUB), lanes]
            slope = slope_all[pl.ds((layer * fold + j) * SUB, SUB), lanes]
            grad = keep(rounded(adjoint * slope), own(j, 0, 1 << 30))
            doubled[j] = grad
            if j < last:
                doubled[fold + j] = pltpu.roll(grad, SUB - 1, 0)
            inner = keep(grad, own(j, -(1 << 30), rows))
            for k in range(TAPS):
                sums[k] = sums[k] + at(last + j - k) * inner
            sums[TAPS] = sums[TAPS] + inner
        for j in range(fold):
            total = c_all[pl.ds(j * SUB, SUB), lanes]
            back = taps[0] * doubled[j]
            for k in range(1, TAPS):
                back = back + taps[k] * doubled[j + k]
            c_all[pl.ds(j * SUB, SUB), lanes] = rounded(total + back)
        for k in range(TAPS + 1):
            g_ref[pl.ds(layer * 5 + k, 1), lanes] = 0.5 * jnp.sum(sums[k], axis=0, keepdims=True)


def window_kernel(rows, layers, x_ref, c_ref, hx_ref, hc_ref, w_ref, b_ref, into_ref, back_ref,
                  out_ref, g_ref, x_all, c_all, slope_all):
    reach, fold, padded = layout_plan(rows, layers)
    width = x_ref.shape[1]
    is_first = lax.axis_index("dp") == 0
    count = fold * SUB
    acts = jnp.concatenate([x_ref[...], hx_ref[...]], axis=0)
    cots = jnp.concatenate([c_ref[...], hc_ref[...]], axis=0)
    x_all[pl.ds((TAPS - 1) * SUB, count), :] = jnp.dot(
        into_ref[...], acts, preferred_element_type=jnp.float32)[:count]
    c_all[...] = jnp.dot(into_ref[...], cots, preferred_element_type=jnp.float32)

    @pl.loop(0, width // LANES)
    def _(chunk):
        lanes = pl.ds(pl.multiple_of(chunk * LANES, LANES), LANES)
        window_chunk(lanes, rows, layers, is_first, w_ref, b_ref, x_all, c_all, slope_all, g_ref)

    out_ref[...] = jnp.dot(
        back_ref[...], c_all[...].astype(jnp.bfloat16), preferred_element_type=jnp.float32
    ).astype(jnp.bfloat16)


def window(acts, cots, halo_acts, halo_cots, weights, bias):
    rows, channels = acts.shape
    layers = weights.shape[0]
    reach, fold, padded = layout_plan(rows, layers)
    width = 512
    into, back = permutations(rows, layers)
    block = lambda *lead: pl.BlockSpec(lead + (width,), lambda i: (0,) * len(lead) + (i,))
    whole = lambda a: pl.BlockSpec(a.shape, lambda i: (0, 0))
    return pl.pallas_call(
        functools.partial(window_kernel, rows, layers),
        grid=(channels // width,),
        out_shape=(
            jax.ShapeDtypeStruct((rows, channels), jnp.bfloat16),
            jax.ShapeDtypeStruct((layers * 5, channels), jnp.float32),
        ),
        in_specs=[
            block(rows), block(rows), block(2 * HALO_ROWS), block(2 * HALO_ROWS),
            block(layers, TAPS), block(layers), whole(into), whole(back),
        ],
        out_specs=(block(rows), block(layers * 5)),
        scratch_shapes=[
            pltpu.VMEM((layers * (fold + TAPS - 1) * SUB, width), jnp.float32),
            pltpu.VMEM((padded, width), jnp.float32),
            pltpu.VMEM((layers * fold * SUB, width), jnp.float32),
        ],
        compiler_params=pltpu.CompilerParams(vmem_limit_bytes=24 << 20),
        cost_estimate=pl.CostEstimate(flops=200_000_000, bytes_accessed=10_000_000, transcendentals=5_000_000),
    )(acts, cots, halo_acts, halo_cots, weights, bias, into, back)


def shifted(value, axis, steps):
    count = lax.axis_size(axis)
    first, final = (max(0, -steps), min(count, count - steps))
    return lax.ppermute(value, axis, [(s, s + steps) for s in range(first, final)])


def inverse_rows(basis, vals):
    channels = basis.shape[-1]
    blocks = basis.reshape(5, 5, channels)
    scale = 1.0 / (vals + 0.1 * jnp.mean(vals))
    return jnp.stack([jnp.sum(blocks[j] * blocks[k] * scale, axis=0) for j, k in PAIRS])


def on_device(query_acts, cotangent, conv_weight, conv_bias, owner_map, basis_store, lambda_store,
              train_grads, batch_index):
    rows, channels = query_acts.shape
    layers = conv_weight.shape[0]
    here = lax.axis_index("dp")
    norm_scale = 1.0 / math.sqrt(rows * lax.axis_size("dp"))
    before = shifted(query_acts[rows - HALO_ROWS:], "dp", 1)
    after = shifted(jnp.concatenate([query_acts[:HALO_ROWS], cotangent[:HALO_ROWS]]), "dp", -1)
    halo_acts = jnp.concatenate([before, after[:HALO_ROWS]])
    halo_cots = jnp.concatenate([jnp.zeros_like(before), after[HALO_ROWS:]])
    own_rows = inverse_rows(basis_store[0], lambda_store[0])
    held = jnp.where((owner_map == here)[:, None, None], own_rows[None], 0.0)
    inverse = lax.psum_scatter(held, "dp", scatter_dimension=2, tiled=True)
    adjoint, partial = window(query_acts, cotangent, halo_acts, halo_cots, conv_weight, conv_bias)
    summed = lax.psum_scatter(partial, "dp", scatter_dimension=1, tiled=True) * norm_scale
    summed = summed.reshape(layers, 5, -1)
    order = {pair: i for i, pair in enumerate(PAIRS)}
    corrected = jnp.stack([
        sum(inverse[:, order[min(j, k), max(j, k)]] * summed[:, k] for k in range(5))
        for j in range(5)
    ], axis=1)
    everyone = lax.all_gather(corrected, "dp", axis=2, tiled=True)
    high = everyone.astype(jnp.bfloat16)
    low = (everyone - high.astype(jnp.float32)).astype(jnp.bfloat16)
    both = high.astype(jnp.float32) + low.astype(jnp.float32)
    examples = train_grads.shape[0]
    values = jnp.sum(train_grads.astype(jnp.float32) * both[None], axis=(1, 2, 3))
    values = values * (1.0 / math.sqrt(5 * layers * channels))
    local_index = batch_index - here * examples
    chosen = local_index[:, None] == jnp.arange(examples, dtype=jnp.int32)[None, :]
    scores = jnp.sum(jnp.where(chosen, values[None, :], 0.0), axis=1)
    return (adjoint, scores)


def solution(mesh):
    in_specs = (
        P(("groups", "dp"), None),
        P(("groups", "dp"), None),
        P(),
        P(),
        P(),
        P("dp", None, None),
        P("dp", None, None),
        P(("groups", "dp"), None, None, None),
        P(("groups", "dp")),
    )
    out_specs = (P(("groups", "dp"), None), P(("groups", "dp")))
    return jax.shard_map(
        on_device, mesh=mesh, in_specs=in_specs, out_specs=out_specs, check_vma=False
    )
```
